32 devices in a mesh: dp: 16 (over z, y, core), mp: 2 (over x).
Axes of the slice: x: 2, y: 2, z: 4, core: 2. Of those that a mesh axis runs over, the one named last changes fastest.
Arguments:
- features: bfloat16 [2048, 4608], P('dp'), may hold values from -6 to 6
- proj_in: bfloat16 [4608, 2560], P('dp', 'mp'), may hold values from -0.09375 to 0.09375
- proj_out: bfloat16 [2560, 2560], P('mp'), may hold values from -0.125 to 0.125
- expert_gate: bfloat16 [64, 2560, 1536], P('dp', None, 'mp'), may hold values from -0.125 to 0.125
- expert_up: bfloat16 [64, 2560, 1536], P('dp', None, 'mp'), may hold values from -0.125 to 0.125
- expert_down: bfloat16 [64, 1536, 2560], P('dp', 'mp'), may hold values from -0.15625 to 0.15625
- routes: int32 [2048, 6], P('dp'), may hold values from 0 to 63, all different within a row; in each aligned block of 128 rows (0 to 127, 128 to 255, ...) at most 15 rows name the same one
- gate_weights: float32 [2048, 6], P('dp'), may hold values from 0.1 to 0.6
- cotangent: bfloat16 [2048, 2560], P('dp'), may hold values from -0.09375 to 0.09375
- first_in: float32 [4608, 2560], P('dp', 'mp'), may hold values from -2 to 2
- second_in: float32 [4608, 2560], P('dp', 'mp'), may hold values from 0.02 to 1
- first_out: float32 [2560, 2560], P('mp', 'dp'), may hold values from -2 to 2
- second_out: float32 [2560, 2560], P('mp', 'dp'), may hold values from 0.02 to 1
Outputs:
- moe_out: bfloat16 [2048, 2560], P('dp')
- new_proj_in: bfloat16 [4608, 2560], P('dp', 'mp')
- new_proj_out: bfloat16 [2560, 2560], P('mp', 'dp')
- new_first_in: float32 [4608, 2560], P('dp', 'mp')
- new_second_in: float32 [4608, 2560], P('dp', 'mp')
- new_first_out: float32 [2560, 2560], P('mp', 'dp')
- new_second_out: float32 [2560, 2560], P('mp', 'dp')
The draws below stay inside these ranges and needn't reach their ends.
Inputs may be any that keep to these rules, and one draw needn't show every extreme that they name: `routes`: each row names 6 different experts. Within the rows of one device (aligned blocks of 128 rows) no expert is named more than 15 times, and in every draw some expert is named exactly 15 times in some block.
All inputs are finite; a program needn't handle non-finite values.
Results may differ from the reference program's by a relative error of at most 0.01.
Values may be sent and summed in bfloat16 or wider, within the bound.
A program may use at most 192 MiB of HBM per device.

```python
import math
import jax
import jax.numpy as jnp
import numpy as np
from jax import lax

VIS = 4608
HID = 2560
D = 2560
EXPERTS = 64
FE = 1536
TOP = 6
TOK_DEV = 128
CAP = 15
TOKENS = 2048
N_DP = 16
N_MP = 2


def steps_of(key, dims, shards, least, largest):
    factor_of = 1.0
    for dim, blocks in shards:
        steps = jax.random.uniform(jax.random.fold_in(jax.random.fold_in(key, 6), dim), (blocks,), jnp.float32, least / len(shards), largest / len(shards))
        factor_of = factor_of * jnp.repeat(jnp.exp(steps), dims[dim] // blocks).reshape((-1,) + (1,) * (len(dims) - 1 - dim))
    return factor_of


def assign_block(rng, own, number, rows, count, top, bound, skew):
    order = jax.random.permutation(rng, count)
    crowded, usual = shares(count, rows * top, bound, skew, True), shares(count, rows * top, bound, skew, False)
    places = jnp.arange(count)

    def named(lengths, rotation):
        used = int((lengths > 0).sum())
        fixed = max(1, used // 4)
        shifted = fixed + (places - fixed + rotation * (used - fixed)) % max(1, count - fixed)
        return jnp.zeros((count,), jnp.int32).at[order[jnp.where(places < fixed, places, shifted)]].set(jnp.asarray(lengths, jnp.int32))

    lengths = jnp.where(number % 4 == 0, named(crowded, number // 4), named(usual, number - number // 4 - 1))
    mixed = jax.random.permutation(jax.random.fold_in(own, 3), count)
    source_of, taker = mixed[0:count // 2 * 2:2], mixed[1:count // 2 * 2:2]
    slack = jnp.minimum(lengths[source_of] - 1, bound - lengths[taker]) // 2
    slack = jnp.where((source_of == order[0]) | (taker == order[0]) | (lengths[taker] == 0), 0, jnp.maximum(slack, 0))
    shifted = jax.random.randint(jax.random.fold_in(own, 4), (count // 2,), 0, 1 << 20) % (slack + 1)
    lengths = lengths.at[source_of].add(-shifted).at[taker].add(shifted)
    labels = jnp.searchsorted(jnp.cumsum(lengths), jnp.arange(rows * top), side="right").astype(jnp.int32)
    table = labels.reshape(top, rows).T
    table = table[jax.random.permutation(jax.random.fold_in(own, 1), rows)]
    rotation = jax.random.randint(jax.random.fold_in(own, 2), (rows, 1), 0, top)
    return jnp.take_along_axis(table, (jnp.arange(top)[None, :] + rotation) % top, axis=1)


def shares(number_of, total, limit, lean, full):
    loads = [(1 << 20) // math.isqrt(standing ** lean) + 1 for standing in range(1, number_of + 1)]
    largest = limit if full else min(limit, max(-(-total // number_of), total * loads[0] // sum(loads)))
    least = 1 if total - largest >= number_of - 1 else 0
    counts, surplus = [largest] + [least] * (number_of - 1), total - largest - least * (number_of - 1)
    while surplus > 0:
        candidates = [i for i in range(1, number_of) if counts[i] < largest] or [i for i in range(1, number_of) if counts[i] < limit]
        mass, remaining = sum([loads[i] for i in candidates]), surplus
        for i in candidates:
            extra = min(limit - counts[i], max(1, remaining * loads[i] // mass), surplus)
            counts[i] = counts[i] + extra
            surplus = surplus - extra
    return np.array(counts)


def scatter_about(stream_key, shape, deviation, most, shards=(), held_as=jnp.bfloat16):
    values = jax.random.normal(stream_key, shape, jnp.float32) * deviation
    if len(shards) > 0:
        values = steps_of(stream_key, shape, shards, -0.22, 0.18) * values
    return jnp.clip(values, min=-most, max=most).astype(held_as)


def setup_inputs(seed: int = 0) -> dict:
    keys = jax.random.split(jax.random.key(seed), 14)
    features = scatter_about(keys[0], (TOKENS, VIS), 1.0, 6.0, ((0, 16),))
    proj_in = scatter_about(keys[1], (VIS, HID), VIS ** -0.5, 0.09375, ((0, 16), (1, 2)))
    proj_out = scatter_about(keys[2], (HID, D), HID ** -0.5, 0.125, ((0, 2),))
    expert_gate = scatter_about(keys[3], (EXPERTS, D, FE), D ** -0.5, 0.125, ((0, 16), (2, 2)))
    expert_up = scatter_about(keys[4], (EXPERTS, D, FE), D ** -0.5, 0.125, ((0, 16), (2, 2)))
    expert_down = scatter_about(keys[5], (EXPERTS, FE, D), FE ** -0.5, 0.15625, ((0, 16), (1, 2)))
    routes_keys = jax.random.split(jax.random.fold_in(keys[6], 1), TOKENS // TOK_DEV)
    routes_turns = jax.random.permutation(jax.random.fold_in(keys[6], 3), TOKENS // TOK_DEV)
    routes = jax.vmap(lambda own, number: assign_block(jax.random.fold_in(keys[6], 2), own, number, TOK_DEV, EXPERTS, TOP, CAP, 2))(routes_keys, routes_turns).reshape((TOKENS, TOP))
    gate_weights = jnp.clip(0.1 + 0.5 * jax.random.uniform(keys[7], (TOKENS, TOP), jnp.float32) ** steps_of(keys[7], (TOKENS, TOP), ((0, 16),), -0.2, 0.2), 0.1, 0.6)
    cotangent = scatter_about(keys[8], (TOKENS, D), 0.015625, 0.09375, ((0, 16),))
    first_in = scatter_about(keys[9], (VIS, HID), 0.3, 2.0, ((0, 16), (1, 2)), jnp.float32)
    second_in = jnp.clip(jnp.exp(math.log(1.0) - 3.912023 * jax.random.uniform(keys[10], (VIS, HID), jnp.float32) ** steps_of(keys[10], (VIS, HID), ((0, 16), (1, 2)), -0.2, 0.2)), 0.02, 1.0)
    first_out = scatter_about(keys[11], (HID, D), 0.3, 2.0, ((0, 2), (1, 16)), jnp.float32)
    second_out = jnp.clip(jnp.exp(math.log(1.0) - 3.912023 * jax.random.uniform(keys[12], (HID, D), jnp.float32) ** steps_of(keys[12], (HID, D), ((0, 2), (1, 16)), -0.2, 0.2)), 0.02, 1.0)
    return {"features": features, "proj_in": proj_in, "proj_out": proj_out, "expert_gate": expert_gate, "expert_up": expert_up, "expert_down": expert_down, "routes": routes, "gate_weights": gate_weights, "cotangent": cotangent, "first_in": first_in, "second_in": second_in, "first_out": first_out, "second_out": second_out}


BETA_ONE = 0.9
BETA_TWO = 0.999
EPSILON = 1e-08
LEARN_RATE = 0.001
WEIGHT_DECAY = 0.1
FIRST_FIX = 1.0 - 0.9 ** 50 * 0.9 ** 50
SECOND_FIX = 1.0 - 0.999 ** 50 * 0.999 ** 50

def gelu_parts(preact):

    def smooth(values):
        return jax.nn.gelu(values, approximate=True)
    result, pullback = jax.vjp(smooth, preact)
    return (result, pullback(jnp.ones_like(preact))[0])

def slot_table(chosen_block):
    chosen = chosen_block.reshape(-1)
    onehot = (chosen[:, None] == jnp.arange(EXPERTS, dtype=jnp.int32)[None, :]).astype(jnp.int32)
    earlier = jnp.cumsum(onehot, axis=0) - onehot
    return (chosen, lax.optimization_barrier(jnp.sum(earlier * onehot, axis=1)).astype(jnp.int32))

def adamw_update(weight, gradient, first, second):
    first_new = BETA_ONE * first + (1.0 - BETA_ONE) * gradient
    second_new = BETA_TWO * second + (1.0 - BETA_TWO) * gradient * gradient
    update = first_new / FIRST_FIX / (jnp.sqrt(second_new / SECOND_FIX) + EPSILON)
    current = weight.astype(jnp.float32)
    return ((current - LEARN_RATE * (update + WEIGHT_DECAY * current)).astype(jnp.bfloat16), first_new, second_new)

def expert_pass(pieces):
    inputs, grads_in, w_gate, w_up, w_down = pieces
    inner_width = w_gate.shape[1] // N_MP
    gate_weight_matrix = w_gate.astype(jnp.float32).reshape(D, N_MP, inner_width)
    up_weight_matrix = w_up.astype(jnp.float32).reshape(D, N_MP, inner_width)
    down_weight_matrix = w_down.astype(jnp.float32).reshape(N_MP, inner_width, D)
    input_wide_rows = inputs.astype(jnp.float32)
    gradient_wide_rows = grads_in.astype(jnp.float32)
    gate_projection = jnp.einsum('ny,yhs->hns', input_wide_rows, gate_weight_matrix)
    up_projection = jnp.einsum('ny,yhs->hns', input_wide_rows, up_weight_matrix)
    sigmoid_gate = jax.nn.sigmoid(gate_projection)
    silu_gate = gate_projection * sigmoid_gate
    inner_activation = (silu_gate * up_projection).astype(jnp.bfloat16)
    output_portions = jnp.einsum('pex,pxi->pei', inner_activation.astype(jnp.float32), down_weight_matrix).astype(jnp.bfloat16)
    down_weight_gradient = jnp.einsum('sb,zab->zsa', gradient_wide_rows, down_weight_matrix)
    gate_weight_gradient = (down_weight_gradient * up_projection * sigmoid_gate * (1.0 + gate_projection * (1.0 - sigmoid_gate))).astype(jnp.bfloat16)
    up_weight_gradient = (down_weight_gradient * silu_gate).astype(jnp.bfloat16)
    input_portions = (jnp.einsum('swv,osv->swo', gate_weight_gradient.astype(jnp.float32), gate_weight_matrix) + jnp.einsum('swv,osv->swo', up_weight_gradient.astype(jnp.float32), up_weight_matrix)).astype(jnp.bfloat16)
    return (lax.optimization_barrier(jnp.sum(output_portions.astype(jnp.float32), axis=0)), lax.optimization_barrier(jnp.sum(input_portions.astype(jnp.float32), axis=0)))

def reference(features, proj_in, proj_out, expert_gate, expert_up, expert_down, routes, gate_weights, cotangent, first_in, second_in, first_out, second_out):
    preact = jnp.dot(features, proj_in, preferred_element_type=jnp.float32)
    activated, gelu_slope = gelu_parts(preact)
    hidden = activated.astype(jnp.bfloat16)
    mapped = jnp.dot(hidden, proj_out, preferred_element_type=jnp.float32).astype(jnp.bfloat16)
    chosen, slot_index = jax.vmap(slot_table)(routes.reshape(N_DP, TOK_DEV, TOP))
    source = jnp.arange(N_DP, dtype=jnp.int32)[:, None]
    position = ((chosen * N_DP + source) * CAP + slot_index).reshape(-1).astype(jnp.int32)
    weights = gate_weights.reshape(-1, 1)
    spread = jnp.repeat(mapped, TOP, axis=0)
    gated_rows = (weights * jnp.repeat(cotangent.astype(jnp.float32), TOP, axis=0)).astype(jnp.bfloat16)
    total_slots = EXPERTS * N_DP * CAP
    slot_inputs = jnp.zeros((total_slots, D), jnp.bfloat16).at[position].set(spread).reshape(EXPERTS, N_DP * CAP, D)
    slot_grads = jnp.zeros((total_slots, D), jnp.bfloat16).at[position].set(gated_rows).reshape(EXPERTS, N_DP * CAP, D)
    expert_outputs, expert_inputs = lax.map(expert_pass, (slot_inputs, slot_grads, expert_gate, expert_up, expert_down))
    back_out = expert_outputs.reshape(total_slots, D)[position]
    back_in = expert_inputs.reshape(total_slots, D)[position]
    moe_out = (mapped.astype(jnp.float32) + lax.optimization_barrier(jnp.sum((weights * back_out).reshape(TOKENS, TOP, D), axis=1))).astype(jnp.bfloat16)
    grad_mapped = (cotangent.astype(jnp.float32) + lax.optimization_barrier(jnp.sum(back_in.reshape(TOKENS, TOP, D), axis=1))).astype(jnp.bfloat16)
    grad_pre = (jnp.dot(grad_mapped, proj_out.T, preferred_element_type=jnp.float32) * gelu_slope).astype(jnp.bfloat16)

    def block_sum(carry, pieces):
        feature_block, pre_block, hidden_block, mapped_block = pieces
        term_in = jnp.dot(feature_block.T, pre_block, preferred_element_type=jnp.float32).astype(jnp.bfloat16)
        term_out = jnp.dot(hidden_block.T, mapped_block, preferred_element_type=jnp.float32).astype(jnp.bfloat16)
        term_in = lax.optimization_barrier(term_in).astype(jnp.float32)
        term_out = lax.optimization_barrier(term_out).astype(jnp.float32)
        return ((carry[0] + term_in, carry[1] + term_out), jnp.zeros((), jnp.float32))
    start_sums = (jnp.zeros((VIS, HID), jnp.float32), jnp.zeros((HID, D), jnp.float32))
    grad_pair, unused = lax.scan(block_sum, start_sums, (features.reshape(N_DP, TOK_DEV, VIS), grad_pre.reshape(N_DP, TOK_DEV, HID), hidden.reshape(N_DP, TOK_DEV, HID), grad_mapped.reshape(N_DP, TOK_DEV, D)))
    new_in, first_in_new, second_in_new = adamw_update(proj_in, grad_pair[0], first_in, second_in)
    new_out, first_out_new, second_out_new = adamw_update(proj_out, grad_pair[1], first_out, second_out)
    return (moe_out, new_in, new_out, first_in_new, second_in_new, first_out_new, second_out_new)
```

```python
import jax
import jax.numpy as jnp
from jax import lax
from jax.sharding import PartitionSpec as P

EXPERTS = 64
TOP = 6
CAP = 15


BETA_ONE = 0.9
BETA_TWO = 0.999
EPSILON = 1e-08
LEARN_RATE = 0.001
WEIGHT_DECAY = 0.1
FIRST_FIX = 1.0 - 0.9**50 * 0.9**50
SECOND_FIX = 1.0 - 0.999**50 * 0.999**50


def gelu_parts(preact):

    def smooth(values):
        return jax.nn.gelu(values, approximate=True)

    result, pullback = jax.vjp(smooth, preact)
    return (result, pullback(jnp.ones_like(preact))[0])


def dispatch_masks(routes, gate_weights, slots):
    rows = routes.shape[0]
    expert_ids = jnp.arange(EXPERTS, dtype=jnp.int32)
    hits = routes.T[:, None, :] == expert_ids[None, :, None]
    named = jnp.any(hits, axis=0)
    weight = jnp.sum(jnp.where(hits, gate_weights.T[:, None, :], 0.0), axis=0)
    before = (jnp.arange(rows)[:, None] < jnp.arange(rows)[None, :]).astype(jnp.bfloat16)
    earlier = jnp.dot(named.astype(jnp.bfloat16), before, preferred_element_type=jnp.float32)
    slot_of = jnp.where(named, earlier.astype(jnp.int32), -1)
    place = slot_of[:, None, :] == jnp.arange(slots, dtype=jnp.int32)[None, :, None]
    weighted = jnp.where(place, weight[:, None, :], 0.0)
    return (
        place.astype(jnp.bfloat16).reshape(EXPERTS * slots, rows),
        weighted.reshape(EXPERTS * slots, rows),
    )


def adamw_update(weight, gradient, first, second):
    first_new = BETA_ONE * first + (1.0 - BETA_ONE) * gradient
    second_new = BETA_TWO * second + (1.0 - BETA_TWO) * gradient * gradient
    update = first_new / FIRST_FIX / (jnp.sqrt(second_new / SECOND_FIX) + EPSILON)
    current = weight.astype(jnp.float32)
    return (
        (current - LEARN_RATE * (update + WEIGHT_DECAY * current)).astype(jnp.bfloat16),
        first_new,
        second_new,
    )


def rows_dot(table, rows):
    return lax.dot_general(
        table, rows, (((0,), (0,)), ((), ())), preferred_element_type=jnp.float32
    )


def local(
    features,
    proj_in,
    proj_out,
    expert_gate,
    expert_up,
    expert_down,
    routes,
    gate_weights,
    cotangent,
    first_in,
    second_in,
    first_out,
    second_out,
):
    row_count = features.shape[0]
    model_width = cotangent.shape[1]
    data_parts = lax.axis_size("dp")
    model_parts = lax.axis_size("mp")
    data_place = lax.axis_index("dp")
    model_place = lax.axis_index("mp")
    column_width = model_width // model_parts
    column_start = model_place * column_width
    own_experts = expert_gate.shape[0]
    slots = -(-CAP // 16) * 16
    expert_rows = data_parts * slots
    width_part = model_width // data_parts

    def exchange(rows):
        blocks = lax.all_to_all(
            rows.reshape(data_parts, own_experts, slots, rows.shape[-1]),
            "dp",
            split_axis=0,
            concat_axis=0,
            tiled=True,
        )
        return blocks.transpose(1, 0, 2, 3).reshape(own_experts, expert_rows, rows.shape[-1])

    def widen(rows):
        return lax.all_gather(rows, "mp", axis=rows.ndim - 1, tiled=True)

    def columns_of(rows):
        return lax.all_to_all(rows, "dp", split_axis=1, concat_axis=0, tiled=True)

    proj_full = lax.all_gather(proj_in, "dp", axis=0, tiled=True)
    place, weighted = dispatch_masks(routes, gate_weights, slots)
    slot_weight = jnp.sum(weighted, axis=1, keepdims=True)
    cotangent_cols = lax.dynamic_slice_in_dim(cotangent, column_start, column_width, 1)
    send_grads = (
        slot_weight * jnp.dot(place, cotangent_cols, preferred_element_type=jnp.float32)
    ).astype(jnp.bfloat16)
    narrow_grads = exchange(send_grads)
    feature_cols = columns_of(features)
    proj_full, narrow_grads, feature_cols = lax.optimization_barrier(
        (proj_full, narrow_grads, feature_cols)
    )

    preact = jnp.dot(features, proj_full, preferred_element_type=jnp.float32)
    activated, gelu_slope = gelu_parts(preact)
    hidden = activated.astype(jnp.bfloat16)
    partial_value = jnp.dot(hidden, proj_out, preferred_element_type=jnp.float32)
    mapped_cols = lax.psum_scatter(partial_value, "mp", scatter_dimension=1, tiled=True).astype(
        jnp.bfloat16
    )
    mapped_cols, narrow_grads = lax.optimization_barrier((mapped_cols, narrow_grads))
    grads_in = widen(narrow_grads)
    send_rows = jnp.dot(place, mapped_cols, preferred_element_type=jnp.float32).astype(
        jnp.bfloat16
    )
    inputs = widen(exchange(send_rows))
    inputs, hidden_sent = lax.optimization_barrier((inputs, hidden))
    hidden_all = lax.all_gather(hidden_sent, "dp", axis=0, tiled=True)

    down_gradient = jnp.einsum(
        "erd,efd->erf", grads_in, expert_down, preferred_element_type=jnp.float32
    )
    gate_value = jnp.einsum("erd,edf->erf", inputs, expert_gate, preferred_element_type=jnp.float32)
    up_value = jnp.einsum("erd,edf->erf", inputs, expert_up, preferred_element_type=jnp.float32)
    sigmoid_gate = jax.nn.sigmoid(gate_value)
    silu_gate = gate_value * sigmoid_gate
    inner = (silu_gate * up_value).astype(jnp.bfloat16)
    gate_gradient = (
        down_gradient * up_value * sigmoid_gate * (1.0 + gate_value * (1.0 - sigmoid_gate))
    ).astype(jnp.bfloat16)
    up_gradient = (down_gradient * silu_gate).astype(jnp.bfloat16)
    input_part = (
        jnp.einsum("erf,edf->erd", gate_gradient, expert_gate, preferred_element_type=jnp.float32)
        + jnp.einsum("erf,edf->erd", up_gradient, expert_up, preferred_element_type=jnp.float32)
    ).astype(jnp.bfloat16)
    inner, input_part = lax.optimization_barrier((inner, input_part))
    out_part = jnp.einsum(
        "erf,efd->erd", inner, expert_down, preferred_element_type=jnp.float32
    ).astype(jnp.bfloat16)

    def narrow(part):
        return lax.psum_scatter(part, "mp", scatter_dimension=2, tiled=True)

    def send_back(part):
        blocks = part.reshape(own_experts, data_parts, slots, column_width)
        return lax.all_to_all(
            blocks.transpose(1, 0, 2, 3), "dp", split_axis=0, concat_axis=0, tiled=True
        ).reshape(EXPERTS * slots, column_width)

    narrow_in = narrow(input_part)
    out_part, narrow_in = lax.optimization_barrier((out_part, narrow_in))
    narrow_out = narrow(out_part)
    back_in = send_back(narrow_in)
    grad_cols = (
        cotangent_cols.astype(jnp.float32) + rows_dot(place, back_in)
    ).astype(jnp.bfloat16)
    grad_mapped = widen(grad_cols)
    grad_hidden = lax.dot_general(
        grad_mapped, proj_out, (((1,), (1,)), ((), ())), preferred_element_type=jnp.float32
    )
    grad_pre = (grad_hidden * gelu_slope).astype(jnp.bfloat16)
    grad_pre, grad_mapped, narrow_out = lax.optimization_barrier(
        (grad_pre, grad_mapped, narrow_out)
    )
    grad_pre_all = lax.all_gather(grad_pre, "dp", axis=0, tiled=True)
    mapped_grad_cols = columns_of(grad_mapped)
    back_out = send_back(narrow_out)
    weight_high = weighted.astype(jnp.bfloat16)
    weight_low = (weighted - weight_high.astype(jnp.float32)).astype(jnp.bfloat16)
    out_cols = (
        mapped_cols.astype(jnp.float32)
        + rows_dot(weight_high, back_out)
        + rows_dot(weight_low, back_out)
    ).astype(jnp.bfloat16)
    moe_out = widen(out_cols)
    grad_out = rows_dot(hidden_all, mapped_grad_cols)
    grad_in = rows_dot(feature_cols, grad_pre_all)
    own_out = lax.dynamic_slice_in_dim(proj_out, data_place * width_part, width_part, 1)
    new_in, first_in_new, second_in_new = adamw_update(proj_in, grad_in, first_in, second_in)
    new_out, first_out_new, second_out_new = adamw_update(own_out, grad_out, first_out, second_out)
    return (moe_out, new_in, new_out, first_in_new, second_in_new, first_out_new, second_out_new)


def solution(mesh):
    return jax.shard_map(
        local,
        mesh=mesh,
        in_specs=(
            P("dp", None),
            P("dp", "mp"),
            P("mp", None),
            P("dp", None, "mp"),
            P("dp", None, "mp"),
            P("dp", "mp", None),
            P("dp", None),
            P("dp", None),
            P("dp", None),
            P("dp", "mp"),
            P("dp", "mp"),
            P("mp", "dp"),
            P("mp", "dp"),
        ),
        out_specs=(
            P("dp", None),
            P("dp", "mp"),
            P("mp", "dp"),
            P("dp", "mp"),
            P("dp", "mp"),
            P("mp", "dp"),
            P("mp", "dp"),
        ),
        check_vma=False,
    )
```

```python
import jax
import jax.numpy as jnp
from jax import lax
from jax.sharding import PartitionSpec as P

EXPERTS = 64
TOP = 6
CAP = 15


BETA_ONE = 0.9
BETA_TWO = 0.999
EPSILON = 1e-08
LEARN_RATE = 0.001
WEIGHT_DECAY = 0.1
FIRST_FIX = 1.0 - 0.9**50 * 0.9**50
SECOND_FIX = 1.0 - 0.999**50 * 0.999**50


def gelu_parts(preact):

    def smooth(values):
        return jax.nn.gelu(values, approximate=True)

    result, pullback = jax.vjp(smooth, preact)
    return (result, pullback(jnp.ones_like(preact))[0])


def dispatch_masks(routes, gate_weights, slots):
    rows = routes.shape[0]
    expert_ids = jnp.arange(EXPERTS, dtype=jnp.int32)
    hits = routes.T[:, None, :] == expert_ids[None, :, None]
    named = jnp.any(hits, axis=0)
    weight = jnp.sum(jnp.where(hits, gate_weights.T[:, None, :], 0.0), axis=0)
    before = (jnp.arange(rows)[:, None] < jnp.arange(rows)[None, :]).astype(jnp.bfloat16)
    earlier = jnp.dot(named.astype(jnp.bfloat16), before, preferred_element_type=jnp.float32)
    slot_of = jnp.where(named, earlier.astype(jnp.int32), -1)
    place = slot_of[:, None, :] == jnp.arange(slots, dtype=jnp.int32)[None, :, None]
    weighted = jnp.where(place, weight[:, None, :], 0.0)
    return (
        place.astype(jnp.bfloat16).reshape(EXPERTS * slots, rows),
        weighted.reshape(EXPERTS * slots, rows),
    )


def adamw_update(weight, gradient, first, second):
    first_new = BETA_ONE * first + (1.0 - BETA_ONE) * gradient
    second_new = BETA_TWO * second + (1.0 - BETA_TWO) * gradient * gradient
    update = first_new / FIRST_FIX / (jnp.sqrt(second_new / SECOND_FIX) + EPSILON)
    current = weight.astype(jnp.float32)
    return (
        (current - LEARN_RATE * (update + WEIGHT_DECAY * current)).astype(jnp.bfloat16),
        first_new,
        second_new,
    )


def rows_dot(table, rows):
    return lax.dot_general(
        table, rows, (((0,), (0,)), ((), ())), preferred_element_type=jnp.float32
    )


def local(
    features,
    proj_in,
    proj_out,
    expert_gate,
    expert_up,
    expert_down,
    routes,
    gate_weights,
    cotangent,
    first_in,
    second_in,
    first_out,
    second_out,
):
    row_count = features.shape[0]
    model_width = cotangent.shape[1]
    data_parts = lax.axis_size("dp")
    model_parts = lax.axis_size("mp")
    data_place = lax.axis_index("dp")
    model_place = lax.axis_index("mp")
    column_width = model_width // model_parts
    column_start = model_place * column_width
    own_experts = expert_gate.shape[0]
    slots = -(-CAP // 16) * 16
    expert_rows = data_parts * slots
    width_part = model_width // data_parts

    def exchange(rows):
        blocks = lax.all_to_all(
            rows.reshape(data_parts, own_experts, slots, rows.shape[-1]),
            "dp",
            split_axis=0,
            concat_axis=0,
            tiled=True,
        )
        return blocks.transpose(1, 0, 2, 3).reshape(own_experts, expert_rows, rows.shape[-1])

    def widen(rows):
        return lax.all_gather(rows, "mp", axis=rows.ndim - 1, tiled=True)

    def columns_of(rows):
        return lax.all_to_all(rows, "dp", split_axis=1, concat_axis=0, tiled=True)

    proj_full = lax.all_gather(proj_in, "dp", axis=0, tiled=True)
    place, weighted = dispatch_masks(routes, gate_weights, slots)
    slot_weight = jnp.sum(weighted, axis=1, keepdims=True)
    cotangent_cols = lax.dynamic_slice_in_dim(cotangent, column_start, column_width, 1)
    send_grads = (
        slot_weight * jnp.dot(place, cotangent_cols, preferred_element_type=jnp.float32)
    ).astype(jnp.bfloat16)
    narrow_grads = exchange(send_grads)
    proj_full, narrow_grads = lax.optimization_barrier((proj_full, narrow_grads))

    preact = jnp.dot(features, proj_full, preferred_element_type=jnp.float32)
    activated, gelu_slope = gelu_parts(preact)
    hidden = activated.astype(jnp.bfloat16)
    partial_value = jnp.dot(hidden, proj_out, preferred_element_type=jnp.float32)
    mapped_cols = lax.psum_scatter(partial_value, "mp", scatter_dimension=1, tiled=True).astype(
        jnp.bfloat16
    )
    mapped_cols, narrow_grads = lax.optimization_barrier((mapped_cols, narrow_grads))
    grads_in = widen(narrow_grads)
    send_rows = jnp.dot(place, mapped_cols, preferred_element_type=jnp.float32).astype(
        jnp.bfloat16
    )
    narrow_rows, features_sent = lax.optimization_barrier((exchange(send_rows), features))
    inputs = widen(narrow_rows)
    feature_cols = columns_of(features_sent)
    inputs, hidden_sent, feature_cols = lax.optimization_barrier((inputs, hidden, feature_cols))
    hidden_all = lax.all_gather(hidden_sent, "dp", axis=0, tiled=True)

    down_gradient = jnp.einsum(
        "erd,efd->erf", grads_in, expert_down, preferred_element_type=jnp.float32
    )
    gate_value = jnp.einsum("erd,edf->erf", inputs, expert_gate, preferred_element_type=jnp.float32)
    up_value = jnp.einsum("erd,edf->erf", inputs, expert_up, preferred_element_type=jnp.float32)
    sigmoid_gate = jax.nn.sigmoid(gate_value)
    silu_gate = gate_value * sigmoid_gate
    inner = (silu_gate * up_value).astype(jnp.bfloat16)
    gate_gradient = (
        down_gradient * up_value * sigmoid_gate * (1.0 + gate_value * (1.0 - sigmoid_gate))
    ).astype(jnp.bfloat16)
    up_gradient = (down_gradient * silu_gate).astype(jnp.bfloat16)
    input_part = (
        jnp.einsum("erf,edf->erd", gate_gradient, expert_gate, preferred_element_type=jnp.float32)
        + jnp.einsum("erf,edf->erd", up_gradient, expert_up, preferred_element_type=jnp.float32)
    ).astype(jnp.bfloat16)
    inner, input_part = lax.optimization_barrier((inner, input_part))
    out_part = jnp.einsum(
        "erf,efd->erd", inner, expert_down, preferred_element_type=jnp.float32
    ).astype(jnp.bfloat16)

    def narrow(part):
        return lax.psum_scatter(part, "mp", scatter_dimension=2, tiled=True)

    def send_back(part):
        blocks = part.reshape(own_experts, data_parts, slots, column_width)
        return lax.all_to_all(
            blocks.transpose(1, 0, 2, 3), "dp", split_axis=0, concat_axis=0, tiled=True
        ).reshape(EXPERTS * slots, column_width)

    narrow_in = narrow(input_part)
    out_part, narrow_in = lax.optimization_barrier((out_part, narrow_in))
    narrow_out = narrow(out_part)
    back_in = send_back(narrow_in)
    grad_cols = (
        cotangent_cols.astype(jnp.float32) + rows_dot(place, back_in)
    ).astype(jnp.bfloat16)
    grad_mapped = widen(grad_cols)
    grad_hidden = lax.dot_general(
        grad_mapped, proj_out, (((1,), (1,)), ((), ())), preferred_element_type=jnp.float32
    )
    grad_pre = (grad_hidden * gelu_slope).astype(jnp.bfloat16)
    grad_pre, grad_mapped, narrow_out = lax.optimization_barrier(
        (grad_pre, grad_mapped, narrow_out)
    )
    grad_pre_all = lax.all_gather(grad_pre, "dp", axis=0, tiled=True)
    mapped_grad_cols = columns_of(grad_mapped)
    back_out = send_back(narrow_out)
    weight_high = weighted.astype(jnp.bfloat16)
    weight_low = (weighted - weight_high.astype(jnp.float32)).astype(jnp.bfloat16)
    out_cols = (
        mapped_cols.astype(jnp.float32)
        + rows_dot(weight_high, back_out)
        + rows_dot(weight_low, back_out)
    ).astype(jnp.bfloat16)
    moe_out = widen(out_cols)
    grad_out = rows_dot(hidden_all, mapped_grad_cols)
    grad_in = rows_dot(feature_cols, grad_pre_all)
    own_out = lax.dynamic_slice_in_dim(proj_out, data_place * width_part, width_part, 1)
    new_in, first_in_new, second_in_new = adamw_update(proj_in, grad_in, first_in, second_in)
    new_out, first_out_new, second_out_new = adamw_update(own_out, grad_out, first_out, second_out)
    return (moe_out, new_in, new_out, first_in_new, second_in_new, first_out_new, second_out_new)


def solution(mesh):
    return jax.shard_map(
        local,
        mesh=mesh,
        in_specs=(
            P("dp", None),
            P("dp", "mp"),
            P("mp", None),
            P("dp", None, "mp"),
            P("dp", None, "mp"),
            P("dp", "mp", None),
            P("dp", None),
            P("dp", None),
            P("dp", None),
            P("dp", "mp"),
            P("dp", "mp"),
            P("mp", "dp"),
            P("mp", "dp"),
        ),
        out_specs=(
            P("dp", None),
            P("dp", "mp"),
            P("mp", "dp"),
            P("dp", "mp"),
            P("dp", "mp"),
            P("mp", "dp"),
            P("mp", "dp"),
        ),
        check_vma=False,
    )
```
